512 devices in a mesh: tm: 16 (over y_hi, x), rows: 16 (over y_lo, z), batch: 2 (over core).
Axes of the slice: x: 4, y: 8 (y_hi: 4, y_lo: 2; y = y_hi * 2 + y_lo), z: 8, core: 2. Of those that a mesh axis runs over, the one named last changes fastest.
Arguments:
- clip_tokens: bfloat16 [2, 64, 32, 28, 512], P('batch', 'tm', 'rows'), may hold values from -6 to 6
- conv_taps: float32 [27, 512], replicated, may hold values from -1 to 1
- norm_gain: float32 [512], replicated, may hold values from 0.5 to 1.5
- heads_weight: bfloat16 [512, 1536], replicated, may hold values from -7.9549513 to 7.9549513
- merge_weight: bfloat16 [512, 512], replicated, may hold values from -0.25 to 0.25
- embed_weight: bfloat16 [512, 128], replicated, may hold values from -0.25 to 0.25
- matches: int32 [2, 64, 32, 28], P('batch', 'tm', 'rows'), may hold values from 0 to 895
- upstream: bfloat16 [2, 64, 32, 28, 512], P('batch', 'tm', 'rows'), may hold values from -6 to 6
Outputs:
- block_out: bfloat16 [2, 64, 32, 28, 512], P('batch', 'tm', 'rows')
- contrast: float32 [2, 64, 32, 28], P('batch', 'tm', 'rows')
- grad_heads: float32 [512, 1536], P(('rows', 'batch'), 'tm')
- grad_gain: float32 [512], replicated
- grad_taps: float32 [27, 512], replicated
The draws below stay inside these ranges and needn't reach their ends.
Inputs may be any that keep to these rules, and one draw needn't show every extreme that they name: matches[c, t, r, w] is row * 28 + column of the patch of frame (t + 4) mod 64 that corresponds to patch (r, w) of frame t.
All inputs are finite; a program needn't handle non-finite values.
Results may differ from the reference program's by a relative error of at most 0.025.
The reference program's roundings to bfloat16 on the way count: a program that leaves them out, or rounds other values in their place, can miss the bound.
Values may be sent and summed in bfloat16 or wider, within the bound.
No kernel may reach another device: no remote copies, remote signals or barrier semaphores. Data moves between devices by JAX's collectives and lax.ppermute only.
A program may use at most 64 MiB of HBM per device.

```python
import math
import jax
import jax.numpy as jnp
from jax import lax

C = 512
HEADS = 8
PD = 128
PW = 28
FR_DEV = 4
TFR = 64
PH = 32
CLIPS = 2


def draw_clip_tokens(key, part):
    key_base = jax.random.fold_in(key, 0)
    shape = (CLIPS, TFR, PH, PW, C)
    values = jax.random.normal(key_base, shape, jnp.float32)
    return jnp.clip(values, -6.0, 6.0).astype(jnp.bfloat16)


def draw_heads_weight(key, part):
    key_query, key_keys, key_values = jax.random.split(key, 3)
    scale = C ** (-0.5)
    query_part = jnp.clip(jax.random.normal(key_query, (C, C), jnp.float32), -4.0, 4.0) * scale
    noise_part = jnp.clip(jax.random.normal(key_keys, (C, C), jnp.float32), -4.0, 4.0) * scale
    value_part = jnp.clip(jax.random.normal(key_values, (C, C), jnp.float32), -4.0, 4.0) * scale
    key_part = noise_part
    return jnp.concatenate([query_part, key_part, value_part], axis=1).astype(jnp.bfloat16)


def touch_ends(values, rng, low, top_value):
    dims = values.shape
    spot = [jax.random.randint(jax.random.fold_in(rng, axis), (), 0, dims[axis]) for axis in range(len(dims))]
    values = values.at[tuple(spot)].set(low)
    longest = dims.index(max(dims))
    spot[longest] = (spot[longest] + 1) % dims[longest]
    return values.at[tuple(spot)].set(top_value)


def level_of(key, extent, pieces, low, largest):
    level = 1.0
    for position, shards_of in pieces:
        steps = jax.random.uniform(jax.random.fold_in(jax.random.fold_in(key, 6), position), (shards_of,), jnp.float32, low / len(pieces), largest / len(pieces))
        level = level * jnp.repeat(jnp.exp(steps), extent[position] // shards_of).reshape((-1,) + (1,) * (len(extent) - 1 - position))
    return level


def scatter_about(key, dims, scale, limit, shards=(), held_as=jnp.bfloat16):
    drawn = jax.random.normal(key, dims, jnp.float32) * scale
    if len(shards) > 0:
        drawn = level_of(key, dims, shards, -0.22, 0.18) * drawn
    return jnp.clip(drawn, min=-limit, max=limit).astype(held_as)


def setup_inputs(seed: int = 0) -> dict:
    seeds = jax.random.split(jax.random.key(seed), 9)
    clip_tokens = draw_clip_tokens(jax.random.fold_in(seeds[8], 71), 0)
    conv_taps = scatter_about(seeds[1], (27, C), 0.2, 1.0, (), jnp.float32)
    norm_gain = jnp.clip(1.0 + 0.1 * jax.random.normal(seeds[2], (C,), jnp.float32), 0.5, 1.5)
    heads_weight = draw_heads_weight(jax.random.fold_in(seeds[8], 71), 0)
    merge_weight = scatter_about(seeds[4], (C, C), C ** -0.5, 0.25)
    embed_weight = scatter_about(seeds[5], (C, PD), C ** -0.5, 0.25)
    matches = touch_ends(jax.random.randint(seeds[6], (CLIPS, TFR, PH, PW), 0, PH * PW), jax.random.fold_in(seeds[6], 1), 0, (PH * PW) - 1).astype(jnp.int32)
    upstream = scatter_about(seeds[7], (CLIPS, TFR, PH, PW, C), 1.0, 6.0, ((0, 2), (1, 16), (2, 16)))
    return dict(clip_tokens=clip_tokens, conv_taps=conv_taps, norm_gain=norm_gain, heads_weight=heads_weight, merge_weight=merge_weight, embed_weight=embed_weight, matches=matches, upstream=upstream)


def depthwise(padded_x, conv_taps, frames, rows):
    width = padded_x.shape[3]
    wide = jnp.pad(padded_x.astype(jnp.float32), ((0, 0), (0, 0), (0, 0), (1, 1), (0, 0)))
    total = jnp.zeros((padded_x.shape[0], frames, rows, width, padded_x.shape[4]), jnp.float32)
    for along_t in range(3):
        for along_r in range(3):
            for along_w in range(3):
                tap = (along_t * 3 + along_r) * 3 + along_w
                total = total + conv_taps[tap] * wide[:, along_t:along_t + frames, along_r:along_r + rows, along_w:along_w + width]
    return total

def taps_grad(padded_x, grad_summed):
    frames, rows, width = (grad_summed.shape[1], grad_summed.shape[2], grad_summed.shape[3])
    wide = jnp.pad(padded_x, ((0, 0), (0, 0), (0, 0), (1, 1), (0, 0)))
    terms = []
    for along_t in range(3):
        for along_r in range(3):
            for along_w in range(3):
                moved = wide[:, along_t:along_t + frames, along_r:along_r + rows, along_w:along_w + width].astype(jnp.float32)
                terms.append(lax.optimization_barrier(jnp.sum(grad_summed * moved, axis=(0, 1, 2, 3))))
    return jnp.stack(terms, axis=0)

def normalize(summed, gain):
    mean_value = lax.optimization_barrier(jnp.mean(summed, axis=-1, keepdims=True))
    centred = summed - mean_value
    variance = lax.optimization_barrier(jnp.mean(centred * centred, axis=-1, keepdims=True))
    inv_std = lax.rsqrt(variance + 1e-05)
    unit = centred * inv_std
    return ((unit * gain).astype(jnp.bfloat16), unit, inv_std)

def window_pass(query, keys_ext, values_ext, grad_att, valid):
    frames = query.shape[1]
    key_win = jnp.stack([keys_ext[:, step:step + frames] for step in range(5)], axis=2).astype(jnp.float32)
    value_win = jnp.stack([values_ext[:, step:step + frames] for step in range(5)], axis=2).astype(jnp.float32)
    query32 = query.astype(jnp.float32)
    grad32 = grad_att.astype(jnp.float32)
    scores = jnp.einsum('bfrwhe,bfdrxhe->bfrhwdx', query32, key_win) * 0.125
    admitted = valid[None, :, None, None, None, :, None]
    scores = jnp.where(admitted, scores, -1e+30)
    top = lax.optimization_barrier(jnp.max(scores, axis=(-2, -1), keepdims=True))
    expo = jnp.exp(scores - top)
    probs = expo / lax.optimization_barrier(jnp.sum(expo, axis=(-2, -1), keepdims=True))
    probs_b = probs.astype(jnp.bfloat16)
    attended = jnp.einsum('bfrhwdx,bfdrxhe->bfrwhe', probs_b.astype(jnp.float32), value_win).astype(jnp.bfloat16)
    grad_prob = jnp.einsum('bfrwhe,bfdrxhe->bfrhwdx', grad32, value_win)
    grad_score = probs * (grad_prob - lax.optimization_barrier(jnp.sum(probs * grad_prob, axis=(-2, -1), keepdims=True)))
    score_b = (grad_score * 0.125).astype(jnp.bfloat16).astype(jnp.float32)
    grad_query = jnp.einsum('bfrhwdx,bfdrxhe->bfrwhe', score_b, key_win).astype(jnp.bfloat16)
    key_terms = jnp.einsum('bfrhwdx,bfrwhe->bfdrxhe', score_b, query32)
    value_terms = jnp.einsum('bfrhwdx,bfrwhe->bfdrxhe', probs_b.astype(jnp.float32), grad32)
    rest = ((0, 0),) * 4
    grad_keys = sum((jnp.pad(key_terms[:, :, step], ((0, 0), (step, 4 - step)) + rest) for step in range(5)))
    grad_values = sum((jnp.pad(value_terms[:, :, step], ((0, 0), (step, 4 - step)) + rest) for step in range(5)))
    return (attended, grad_query, grad_keys, grad_values)

def reference(clip_tokens, conv_taps, norm_gain, heads_weight, merge_weight, embed_weight, matches, upstream):
    clips, frames, rows, width, chans = clip_tokens.shape
    head_size = chans // HEADS
    padded = jnp.pad(clip_tokens, ((0, 0), (1, 1), (1, 1), (0, 0), (0, 0)))
    summed = clip_tokens.astype(jnp.float32) + depthwise(padded, conv_taps, frames, rows)
    normed, unit, inv_std = normalize(summed, norm_gain)
    flat = normed.reshape(-1, chans)
    packed = jnp.dot(flat, heads_weight, preferred_element_type=jnp.float32).astype(jnp.bfloat16)
    grad_att = jnp.dot(upstream.reshape(-1, chans), merge_weight.T, preferred_element_type=jnp.float32).astype(jnp.bfloat16)
    six = (clips, frames, rows, width, HEADS, head_size)
    frame_pad = ((0, 0), (2, 2), (0, 0), (0, 0), (0, 0), (0, 0))
    query = packed[:, :chans].reshape(six)
    keys_ext = jnp.pad(packed[:, chans:2 * chans].reshape(six), frame_pad)
    values_ext = jnp.pad(packed[:, 2 * chans:].reshape(six), frame_pad)
    grad_six = grad_att.reshape(six)
    frame_ids = jnp.arange(frames)[:, None] + jnp.arange(5)[None, :] - 2
    valid = (frame_ids >= 0) & (frame_ids < frames)
    block = math.gcd(rows, 4)
    count = rows // block

    def split(array):
        shape = array.shape
        return jnp.moveaxis(array.reshape(shape[:2] + (count, block) + shape[3:]), 2, 0)

    def merge(array):
        moved = jnp.moveaxis(array, 0, 2)
        shape = moved.shape
        return moved.reshape(shape[:2] + (count * block,) + shape[4:])

    def per_block(items):
        return window_pass(items[0], items[1], items[2], items[3], valid)
    outs = lax.map(per_block, (split(query), split(keys_ext), split(values_ext), split(grad_six)))
    attended, grad_query, grad_keys, grad_values = [merge(item) for item in outs]
    mixed = jnp.dot(attended.reshape(-1, chans), merge_weight, preferred_element_type=jnp.float32)
    block_out = (summed + mixed.reshape(summed.shape)).astype(jnp.bfloat16)
    embed = jnp.dot(block_out.reshape(-1, chans), embed_weight, preferred_element_type=jnp.float32).astype(jnp.bfloat16)
    embed = embed.reshape(clips, frames, rows * width, -1)
    partner = jnp.roll(embed, -FR_DEV, axis=1)
    wanted = matches.reshape(clips, frames, rows * width).astype(jnp.int32)
    picked = jnp.take_along_axis(partner, wanted[..., None], axis=2)
    differ = embed.astype(jnp.float32) - picked.astype(jnp.float32)
    contrast = lax.optimization_barrier(jnp.mean(differ * differ, axis=-1)).reshape(clips, frames, rows, width)
    grad_key = grad_keys[:, 2:frames + 2].astype(jnp.bfloat16).reshape(-1, chans)
    grad_value = grad_values[:, 2:frames + 2].astype(jnp.bfloat16).reshape(-1, chans)
    grad_packed = jnp.concatenate([grad_query.reshape(-1, chans), grad_key, grad_value], axis=1)
    grad_heads = jnp.dot(flat.T, grad_packed, preferred_element_type=jnp.float32)
    grad_normed = jnp.dot(grad_packed, heads_weight.T, preferred_element_type=jnp.float32).reshape(summed.shape)
    grad_gain = lax.optimization_barrier(jnp.sum(grad_normed * unit, axis=(0, 1, 2, 3)))
    scaled = grad_normed * norm_gain
    grad_summed = upstream.astype(jnp.float32) + inv_std * (scaled - lax.optimization_barrier(jnp.mean(scaled, axis=-1, keepdims=True)) - unit * lax.optimization_barrier(jnp.mean(scaled * unit, axis=-1, keepdims=True)))
    grad_taps = taps_grad(padded, grad_summed)
    return (block_out, contrast, grad_heads, grad_gain, grad_taps)
```

```python
import jax
import jax.numpy as jnp
import numpy as np
from jax import lax
from jax.experimental import pallas as pl
from jax.experimental.pallas import tpu as pltpu
from jax.sharding import Mesh, PartitionSpec as P

F32 = jnp.float32
BF16 = jnp.bfloat16
W = 28
WP = 32
C = 512
TM = ("yh", "x")
ROWS = ("yl", "z")

NN = (((1,), (0,)), ((), ()))
NT = (((1,), (1,)), ((), ()))
TN = (((0,), (0,)), ((), ()))


def mm(a, b, dims):
    return lax.dot_general(a, b, dims, preferred_element_type=F32)


def attend_kernel(
    tm_ref, own_ref, prev_ref, next_ref, up_ref, down_ref, taps_ref, gain_ref, heads_ref,
    merge_ref, upstream_ref,
    summed_ref, unit_ref, inv_ref, normed_ref, tokens_ref, grad_ref, att_ref, dq_ref, dkv_ref,
    owed_prev_ref, owed_next_ref,
    xs, ns, qs, kvs, gs, bias_s,
):
    zeros_tail = jnp.zeros((8, C), F32)

    def place(f, row, slab):
        xs[f, row, 24:32, :] = zeros_tail
        xs[f, row, 0:W, :] = slab.astype(F32)

    for f in range(3):
        for r in range(2):
            place(f, 1 + r, prev_ref[f, r])
            place(7 + f, 1 + r, next_ref[f, r])
    for f in range(4):
        for r in range(2):
            place(3 + f, 1 + r, own_ref[f, r])
    for f in range(10):
        place(f, 0, up_ref[f])
        place(f, 3, down_ref[f])
    for f in range(6):
        for row in range(4):
            tokens_ref[f, row] = xs[f + 2, row].astype(BF16)

    keep = lax.broadcasted_iota(jnp.int32, (WP, 1), 0) < W

    grad_ref[...] = jnp.zeros(grad_ref.shape, BF16)
    for f in range(4):
        for r in range(2):
            grad_ref[r, f * WP : f * WP + W, :] = upstream_ref[f, r]

    def conv_frame(f, carry):
        for r in range(2):
            parts = []
            for c in range(4):
                lanes = slice(c * 128, (c + 1) * 128)
                acc = [None, None, None]
                centre = None
                for dt in range(3):
                    for dr in range(3):
                        slab = xs[f + dt, r + dr, :, lanes]
                        if dt == 1 and dr == 1:
                            centre = slab
                        for dw in range(3):
                            tap = (dt * 3 + dr) * 3 + dw
                            term = taps_ref[tap : tap + 1, lanes] * slab
                            acc[dw] = term if acc[dw] is None else acc[dw] + term
                total = acc[1] + pltpu.roll(acc[0], 1, 0) + pltpu.roll(acc[2], WP - 1, 0)
                parts.append(centre + total)
            summed = jnp.concatenate(parts, axis=1)
            mean = jnp.sum(summed, axis=1, keepdims=True) * (1.0 / C)
            centred = summed - mean
            var = jnp.sum(centred * centred, axis=1, keepdims=True) * (1.0 / C)
            inv = lax.rsqrt(var + 1e-05)
            unit = jnp.where(keep, centred * inv, 0.0)
            normed = (unit * gain_ref[...]).astype(BF16)
            ns[r, pl.ds(pl.multiple_of(f * WP, WP), WP), :] = normed

            @pl.when((f >= 2) & (f < 6))
            def _():
                rows = pl.ds(pl.multiple_of((f - 2) * WP, WP), WP)
                summed_ref[r, rows, :] = summed
                unit_ref[r, rows, :] = unit
                inv_ref[r, rows, :] = jnp.broadcast_to(inv, (WP, 128))

        return carry

    lax.fori_loop(0, 8, conv_frame, 0)

    for r in range(2):
        own = ns[r, 64:192, :]
        normed_ref[r] = own
        kvs[r] = mm(ns[r], heads_ref[:, C:], NN).astype(BF16)
        qs[r] = (mm(own, heads_ref[:, :C], NN).astype(BF16).astype(F32) * 0.125).astype(BF16)
        gs[r] = mm(grad_ref[r], merge_ref[...], NT).astype(BF16)

    q_at = lax.broadcasted_iota(jnp.int32, (256, 256), 0)
    k_at = lax.broadcasted_iota(jnp.int32, (256, 256), 1)
    q_frame = (q_at >> 5) & 3
    k_frame = k_at >> 5
    tm = tm_ref[0]
    ok = (k_frame >= q_frame) & (k_frame <= q_frame + 4) & ((k_at & 31) < W)
    ok = ok & ((k_frame >= 2) | (tm > 0)) & ((k_frame < 6) | (tm < tm_ref[1] - 1))
    bias_s[...] = jnp.where(ok, 0.0, -1e30)
    lane = lax.broadcasted_iota(jnp.int32, (1, 128), 1)
    low = (lane < 64).astype(F32).astype(BF16)
    high = (lane >= 64).astype(F32).astype(BF16)
    low_lane = lane < 64

    def head_pair(it, carry):
        r = it // 4
        p = it % 4
        lanes = pl.ds(pl.multiple_of(p * 128, 128), 128)
        vlanes = pl.ds(pl.multiple_of(C + p * 128, 128), 128)
        q = qs[r, :, lanes]
        g = gs[r, :, lanes]
        k = kvs[r, :, lanes]
        v = kvs[r, :, vlanes]
        qq = jnp.concatenate([q * low, q * high], axis=0)
        gg = jnp.concatenate([g * low, g * high], axis=0)
        s = mm(qq, k, NT) + bias_s[...]
        gp = mm(gg, v, NT)
        e = jnp.exp(s - jnp.max(s, axis=1, keepdims=True))
        prob = e * (1.0 / jnp.sum(e, axis=1, keepdims=True))
        pb = prob.astype(BF16)
        pg = prob * gp
        ds = (pg - prob * jnp.sum(pg, axis=1, keepdims=True)).astype(BF16)
        o = mm(pb, v, NN)
        att_ref[r, :, lanes] = jnp.where(low_lane, o[:128], o[128:]).astype(BF16)
        dq = mm(ds, k, NN) * 0.125
        dq_ref[r, :, lanes] = jnp.where(low_lane, dq[:128], dq[128:]).astype(BF16)
        dk = mm(ds, qq, TN)
        dv = mm(pb, gg, TN)
        for value, at in ((dk, lanes), (dv, vlanes)):
            owed_prev_ref[r, :, at] = value[:64].astype(BF16)
            dkv_ref[r, :, at] = value[64:192]
            owed_next_ref[r, :, at] = value[192:].astype(BF16)
        return carry

    lax.fori_loop(0, 8, head_pair, 0)


def merge_kernel(att_ref, summed_ref, merge_ref, embed_w_ref, out_ref, embed_ref):
    for r in range(2):
        mixed = mm(att_ref[r], merge_ref[...], NN)
        block = (summed_ref[r] + mixed).astype(BF16)
        embed = mm(block, embed_w_ref[...], NN).astype(BF16)
        for f in range(4):
            out_ref[f, r] = block[f * WP : f * WP + W]
            embed_ref[f, r * WP : (r + 1) * WP, :] = embed[f * WP : (f + 1) * WP]


def grads_kernel(
    dkv_ref, from_prev_ref, from_next_ref, dq_ref, normed_ref, heads_ref, gain_ref, unit_ref,
    inv_ref, grad_ref, tokens_ref,
    out_ref, gp, shifts, red,
):
    for r in range(2):
        rows = slice(r * 128, (r + 1) * 128)
        gp[rows, 0:C] = dq_ref[r]
        gp[r * 128 : r * 128 + 64, C:] = (
            dkv_ref[r, 0:64, :] + from_prev_ref[r].astype(F32)
        ).astype(BF16)
        gp[r * 128 + 64 : (r + 1) * 128, C:] = (
            dkv_ref[r, 64:128, :] + from_next_ref[r].astype(F32)
        ).astype(BF16)

    col = lax.broadcasted_iota(jnp.int32, (C, C), 1)
    row = lax.broadcasted_iota(jnp.int32, (C, C), 0)
    source = ((col >> 4) & 15) * 32 + (col >> 8) * 16 + (col & 15)
    perm = (row == source).astype(F32).astype(BF16)
    normed = normed_ref[...].reshape(256, C)
    ordered = mm(normed, perm, NN).astype(BF16)
    for yh in range(4):
        part = mm(gp[:, yh * 384 : (yh + 1) * 384], ordered, TN).astype(BF16)
        for x in range(4):
            at = (x * 4 + yh) * 96
            for b in range(2):
                out_ref[b, at : at + 96, :] = part[x * 96 : (x + 1) * 96, b * 256 : (b + 1) * 256]

    gn = mm(gp[...], heads_ref[...], NT)
    unit = unit_ref[...].reshape(256, C)
    inv = inv_ref[...].reshape(256, 128)[:, 0:1]
    gu = gn * unit
    gain_sum = jnp.sum(gu.reshape(32, 8, C), axis=0)
    gain = gain_ref[...]
    scaled = gn * gain
    mean_a = jnp.sum(scaled, axis=1, keepdims=True) * (1.0 / C)
    mean_b = jnp.sum(gu * gain, axis=1, keepdims=True) * (1.0 / C)
    grad = grad_ref[...].reshape(256, C).astype(F32) + inv * (scaled - mean_a - unit * mean_b)
    keep = (lax.broadcasted_iota(jnp.int32, (256, 1), 0) & 31) < W
    grad = jnp.where(keep, grad, 0.0)
    for slab in range(8):
        piece = grad[slab * WP : (slab + 1) * WP]
        shifts[0, slab] = pltpu.roll(piece, WP - 1, 0)
        shifts[1, slab] = piece
        shifts[2, slab] = pltpu.roll(piece, 1, 0)

    def lane_chunk(c, carry):
        lanes = pl.ds(pl.multiple_of(c * 128, 128), 128)
        for dw in range(3):
            acc = [jnp.zeros((8, 128), F32) for _ in range(9)]
            for slab in range(8):
                r, f = slab // 4, slab % 4
                piece = shifts[dw, slab, :, lanes]
                for dt in range(3):
                    for dr in range(3):
                        token = tokens_ref[f + dt, r + dr, :, lanes].astype(F32)
                        prod = piece * token
                        acc[dt * 3 + dr] = acc[dt * 3 + dr] + (
                            (prod[0:8] + prod[8:16]) + (prod[16:24] + prod[24:32])
                        )
            for k in range(9):
                red[pl.ds((k * 3 + dw), 1), lanes] = jnp.sum(acc[k], axis=0, keepdims=True)
        return carry

    red[24:32, :] = jnp.zeros((8, C), F32)
    lax.fori_loop(0, 4, lane_chunk, 0)
    red[27:28, :] = jnp.sum(gain_sum, axis=0, keepdims=True)
    value = red[...]
    hi = value.astype(BF16)
    lo = (value - hi.astype(F32)).astype(BF16)
    for b in range(2):
        for half in range(2):
            at = slice(half * 256, (half + 1) * 256)
            out_ref[b, 1536 + half * 32 : 1568 + half * 32, :] = hi[:, at]
            out_ref[b, 1600 + half * 32 : 1632 + half * 32, :] = lo[:, at]


def split_pair(value):
    hi = value.astype(BF16)
    return hi, (value - hi.astype(F32)).astype(BF16)


def reduce_b_kernel(in_ref, out_ref):
    hi, lo = split_pair(
        (in_ref[0, 1536:1600].astype(F32) + in_ref[0, 1600:1664].astype(F32))
        + (in_ref[1, 1536:1600].astype(F32) + in_ref[1, 1600:1664].astype(F32))
    )
    for x in range(4):
        rows = slice(x * 384, (x + 1) * 384)
        out_ref[x, 0:384, :] = (
            in_ref[0, rows].astype(F32) + in_ref[1, rows].astype(F32)
        ).astype(BF16)
        out_ref[x, 384:448, :] = hi
        out_ref[x, 448:512, :] = lo


def reduce_x_kernel(in_ref, out_ref):
    parts = [in_ref[x].astype(F32) for x in range(4)]
    total = (parts[0] + parts[1]) + (parts[2] + parts[3])
    heads = total[0:384].astype(BF16)
    small = total[384:448] + total[448:512]
    for yh in range(4):
        for yl in range(2):
            k = yh * 2 + yl
            out_ref[k, 0:96, :] = heads[yh * 96 : (yh + 1) * 96, yl * 128 : (yl + 1) * 128]
            for half in range(2):
                hi, lo = split_pair(small[k * 8 : (k + 1) * 8, half * 128 : (half + 1) * 128])
                out_ref[k, 96 + half * 8 : 104 + half * 8, :] = hi
                out_ref[k, 112 + half * 8 : 120 + half * 8, :] = lo


def reduce_y_kernel(in_ref, out_ref):
    total = in_ref[0].astype(F32)
    for k in range(1, 8):
        total = total + in_ref[k].astype(F32)
    turned = jnp.transpose(total)
    hi, lo = split_pair(total[96:112] + total[112:128])
    for z in range(8):
        out_ref[z, 0:16, :] = turned[z * 16 : (z + 1) * 16, :].astype(BF16)
        out_ref[z, 16:32, :] = hi
        out_ref[z, 32:48, :] = lo


def reduce_z_kernel(in_ref, heads_ref, small_ref):
    total = in_ref[0].astype(F32)
    for k in range(1, 8):
        total = total + in_ref[k].astype(F32)
    heads_ref[...] = total[0:16, 0:96]
    small = total[16:32] + total[32:48]
    for k in range(8):
        small_ref[k] = small


def spread_kernel(in_ref, gain_ref, taps_ref, tmp):
    for k in range(8):
        for half in range(2):
            lanes = slice((k // 4) * 256 + half * 128, (k // 4) * 256 + half * 128 + 128)
            tmp[(k % 4) * 8 : (k % 4) * 8 + 8, lanes] = in_ref[k, half * 8 : half * 8 + 8, :]
    gain_ref[...] = tmp[27:28, :]
    taps_ref[...] = tmp[0:27, :]


def contrast_kernel(pos_ref, match_ref, embed_ref, g0_ref, g1_ref, g2_ref, g3_ref, out_ref):
    own = pos_ref[0]
    at = lax.broadcasted_iota(jnp.int32, (1024, W), 0)
    ones = jnp.ones((8, 128), F32)
    for f in range(4):
        table = jnp.concatenate(
            [g0_ref[:, f].reshape(128, 128), g1_ref[:, f].reshape(128, 128)]
            + [g2_ref[:, f].reshape(256, 128), g3_ref[:, f].reshape(512, 128)],
            axis=0,
        )
        for r in range(2):
            match = match_ref[f, r : r + 1, :]
            row = (match * 2341) >> 16
            wcol = match - row * W
            block = (row >> 1) ^ own
            where = ((block & 7) * 2 + (block >> 3)) * 64 + (row & 1) * WP + wcol
            pick = (at == where).astype(F32).astype(BF16)
            found = mm(pick, table, TN)
            differ = embed_ref[f, r * WP : r * WP + W, :].astype(F32) - found
            square = differ * differ
            res = lax.dot_general(
                ones, square, NT, precision=lax.Precision.HIGHEST, preferred_element_type=F32
            )
            out_ref[f, r : r + 1, :] = res[0:1, :] * (1.0 / 128.0)


def sds(shape, dtype):
    return jax.ShapeDtypeStruct(shape, dtype)


def smem():
    return pl.BlockSpec(memory_space=pltpu.SMEM)


def vmem():
    return pl.BlockSpec(memory_space=pltpu.VMEM)


def call(kernel, outs, ins, smem_first=False, scratch=(), name=None):
    specs = [vmem() for _ in ins]
    if smem_first:
        specs[0] = smem()
    return pl.pallas_call(
        kernel,
        out_shape=outs,
        in_specs=specs,
        out_specs=jax.tree.map(lambda _: vmem(), outs),
        scratch_shapes=list(scratch),
        compiler_params=pltpu.CompilerParams(vmem_limit_bytes=48 * 1024 * 1024),
        name=name,
    )(*ins)


def moved(block, axis, route):
    return lax.ppermute(block, axis, route)


def on_device(
    clip_tokens, conv_taps, norm_gain, heads_weight, merge_weight, embed_weight, matches, upstream
):
    tokens = clip_tokens[0]
    tm = lax.axis_index(TM)
    rows = lax.axis_index(ROWS)
    n_tm = lax.axis_size(TM)
    n_rows = lax.axis_size(ROWS)
    fwd = [(i, i + 1) for i in range(n_tm - 1)]
    back = [(i + 1, i) for i in range(n_tm - 1)]
    down = [(i, i + 1) for i in range(n_rows - 1)]
    up = [(i + 1, i) for i in range(n_rows - 1)]
    prev3 = moved(tokens[1:4], TM, fwd)
    next3 = moved(tokens[0:3], TM, back)
    last = jnp.concatenate([prev3[:, 1], tokens[:, 1], next3[:, 1]], axis=0)
    first = jnp.concatenate([prev3[:, 0], tokens[:, 0], next3[:, 0]], axis=0)
    above = moved(last, ROWS, down)
    below = moved(first, ROWS, up)
    gain = norm_gain.reshape(1, C)
    ups = upstream[0]
    where_tm = jnp.stack([tm, jnp.int32(n_tm)]).astype(jnp.int32)

    outs = (
        sds((2, 128, C), F32),
        sds((2, 128, C), F32),
        sds((2, 128, 128), F32),
        sds((2, 128, C), BF16),
        sds((6, 4, WP, C), BF16),
        sds((2, 128, C), BF16),
        sds((2, 128, C), BF16),
        sds((2, 128, C), BF16),
        sds((2, 128, 2 * C), F32),
        sds((2, 64, 2 * C), BF16),
        sds((2, 64, 2 * C), BF16),
    )
    summed, unit, inv, normed, tok6, grad, att, dq, dkv, owed_prev, owed_next = call(
        attend_kernel,
        outs,
        (where_tm, tokens, prev3, next3, above, below, conv_taps, gain, heads_weight,
         merge_weight, ups),
        smem_first=True,
        scratch=(
            pltpu.VMEM((10, 4, WP, C), F32),
            pltpu.VMEM((2, 256, C), BF16),
            pltpu.VMEM((2, 128, C), BF16),
            pltpu.VMEM((2, 256, 2 * C), BF16),
            pltpu.VMEM((2, 128, C), BF16),
            pltpu.VMEM((256, 256), F32),
        ),
        name="attend",
    )
    from_next = moved(owed_prev, TM, back)
    from_prev = moved(owed_next, TM, fwd)

    block_out, embed = call(
        merge_kernel,
        (sds((4, 2, W, C), BF16), sds((4, 64, 128), BF16)),
        (att, summed, merge_weight, embed_weight),
        name="merge",
    )
    grid = ("yh", "x", "yl", "z")
    n_z = lax.axis_size("z")
    n_yl = lax.axis_size("yl")
    spots = [(t, q) for t in range(n_tm) for q in range(n_rows)]
    same = [(t * n_rows + q, ((t - 1) % n_tm) * n_rows + q) for t, q in spots]
    other = [
        (t * n_rows + q, ((t - 1) % n_tm) * n_rows + (q + n_z) % n_rows) for t, q in spots
    ]
    near = moved(embed, grid, same)
    far = moved(embed, grid, other)

    (stage,) = call(
        grads_kernel,
        (sds((2, 1664, 256), BF16),),
        (dkv, from_prev, from_next, dq, normed, heads_weight, gain, unit, inv, grad, tok6),
        scratch=(
            pltpu.VMEM((256, 3 * C), BF16),
            pltpu.VMEM((3, 8, WP, C), F32),
            pltpu.VMEM((32, C), F32),
        ),
        name="grads",
    )

    def swap(block, bit):
        return moved(block, "z", [(i, i ^ bit) for i in range(n_z)])

    stage, near, far = lax.optimization_barrier((stage, near, far))
    g0 = jnp.stack([near, far])
    g1 = swap(g0, 1)
    stage, g0 = lax.optimization_barrier((stage, g0))
    stage = lax.all_to_all(stage, "b", 0, 0, tiled=True)
    (stage,) = call(reduce_b_kernel, (sds((4, 512, 256), BF16),), (stage,), name="sum_b")
    stage, g1 = lax.optimization_barrier((stage, g1))
    g01 = jnp.concatenate([g0, g1], axis=0)
    g2 = swap(g01, 2)
    stage, g01 = lax.optimization_barrier((stage, g01))
    stage = lax.all_to_all(stage, "x", 0, 0, tiled=True)
    (stage,) = call(reduce_x_kernel, (sds((8, 128, 128), BF16),), (stage,), name="sum_x")
    stage, g2 = lax.optimization_barrier((stage, g2))
    g03 = jnp.concatenate([g01, g2], axis=0)
    g3 = swap(g03, 4)
    stage, g03 = lax.optimization_barrier((stage, g03))
    stage = lax.all_to_all(stage, ("yh", "yl"), 0, 0, tiled=True)
    (stage,) = call(reduce_y_kernel, (sds((8, 48, 128), BF16),), (stage,), name="sum_y")
    stage = lax.all_to_all(stage, "z", 0, 0, tiled=True)
    grad_heads, small = call(
        reduce_z_kernel, (sds((16, 96), F32), sds((8, 16, 128), F32)), (stage,), name="sum_z"
    )
    small = lax.all_to_all(small, ("yh", "yl"), 0, 0, tiled=True)
    grad_gain, grad_taps = call(
        spread_kernel,
        (sds((1, C), F32), sds((27, C), F32)),
        (small,),
        scratch=(pltpu.VMEM((32, C), F32),),
        name="spread",
    )
    small, g3 = lax.optimization_barrier((small, g3))
    (contrast,) = call(
        contrast_kernel,
        (sds((4, 2, W), F32),),
        (rows.reshape(1).astype(jnp.int32), matches[0], embed, g0, g1, g2, g3),
        smem_first=True,
        name="contrast",
    )
    return (block_out[None], contrast[None], grad_heads, grad_gain.reshape(C), grad_taps)


def solution(mesh):
    fine = Mesh(
        np.asarray(mesh.devices).reshape(4, 4, 2, 8, 2), ("yh", "x", "yl", "z", "b")
    )
    placed = (
        P("b", TM, ROWS, None, None),
        P(),
        P(),
        P(),
        P(),
        P(),
        P("b", TM, ROWS, None),
        P("b", TM, ROWS, None, None),
    )
    return jax.shard_map(
        on_device,
        mesh=fine,
        in_specs=placed,
        out_specs=(
            P("b", TM, ROWS, None, None),
            P("b", TM, ROWS, None),
            P(("yl", "z", "b"), TM),
            P(),
            P(),
        ),
        check_vma=False,
    )
```

```python
import jax
import jax.numpy as jnp
import numpy as np
from jax import lax
from jax.experimental import pallas as pl
from jax.experimental.pallas import tpu as pltpu
from jax.sharding import Mesh, PartitionSpec as P

F32 = jnp.float32
BF16 = jnp.bfloat16
W = 28
WP = 32
C = 512
TM = ("yh", "x")
ROWS = ("yl", "z")

NN = (((1,), (0,)), ((), ()))
NT = (((1,), (1,)), ((), ()))
TN = (((0,), (0,)), ((), ()))


def mm(a, b, dims):
    return lax.dot_general(a, b, dims, preferred_element_type=F32)


def attend_kernel(
    tm_ref, own_ref, prev_ref, next_ref, up_ref, down_ref, taps_ref, gain_ref, heads_ref,
    merge_ref, upstream_ref,
    summed_ref, unit_ref, inv_ref, normed_ref, tokens_ref, grad_ref, att_ref, dq_ref, dkv_ref,
    owed_prev_ref, owed_next_ref,
    xs, ns, qs, kvs, gs, bias_s,
):
    zeros_tail = jnp.zeros((8, C), F32)

    def place(f, row, slab):
        xs[f, row, 24:32, :] = zeros_tail
        xs[f, row, 0:W, :] = slab.astype(F32)

    for f in range(3):
        for r in range(2):
            place(f, 1 + r, prev_ref[f, r])
            place(7 + f, 1 + r, next_ref[f, r])
    for f in range(4):
        for r in range(2):
            place(3 + f, 1 + r, own_ref[f, r])
    for f in range(10):
        place(f, 0, up_ref[f])
        place(f, 3, down_ref[f])
    for f in range(6):
        for row in range(4):
            tokens_ref[f, row] = xs[f + 2, row].astype(BF16)

    keep = lax.broadcasted_iota(jnp.int32, (WP, 1), 0) < W

    grad_ref[...] = jnp.zeros(grad_ref.shape, BF16)
    for f in range(4):
        for r in range(2):
            grad_ref[r, f * WP : f * WP + W, :] = upstream_ref[f, r]

    def conv_frame(f, carry):
        for r in range(2):
            parts = []
            for c in range(4):
                lanes = slice(c * 128, (c + 1) * 128)
                acc = [None, None, None]
                centre = None
                for dt in range(3):
                    for dr in range(3):
                        slab = xs[f + dt, r + dr, :, lanes]
                        if dt == 1 and dr == 1:
                            centre = slab
                        for dw in range(3):
                            tap = (dt * 3 + dr) * 3 + dw
                            term = taps_ref[tap : tap + 1, lanes] * slab
                            acc[dw] = term if acc[dw] is None else acc[dw] + term
                total = acc[1] + pltpu.roll(acc[0], 1, 0) + pltpu.roll(acc[2], WP - 1, 0)
                parts.append(centre + total)
            summed = jnp.concatenate(parts, axis=1)
            mean = jnp.sum(summed, axis=1, keepdims=True) * (1.0 / C)
            centred = summed - mean
            var = jnp.sum(centred * centred, axis=1, keepdims=True) * (1.0 / C)
            inv = lax.rsqrt(var + 1e-05)
            unit = jnp.where(keep, centred * inv, 0.0)
            normed = (unit * gain_ref[...]).astype(BF16)
            ns[r, pl.ds(pl.multiple_of(f * WP, WP), WP), :] = normed

            @pl.when((f >= 2) & (f < 6))
            def _():
                rows = pl.ds(pl.multiple_of((f - 2) * WP, WP), WP)
                summed_ref[r, rows, :] = summed
                unit_ref[r, rows, :] = unit
                inv_ref[r, rows, :] = jnp.broadcast_to(inv, (WP, 128))

        return carry

    lax.fori_loop(0, 8, conv_frame, 0)

    for r in range(2):
        own = ns[r, 64:192, :]
        normed_ref[r] = own
        kvs[r] = mm(ns[r], heads_ref[:, C:], NN).astype(BF16)
        qs[r] = (mm(own, heads_ref[:, :C], NN).astype(BF16).astype(F32) * 0.125).astype(BF16)
        gs[r] = mm(grad_ref[r], merge_ref[...], NT).astype(BF16)

    q_at = lax.broadcasted_iota(jnp.int32, (256, 256), 0)
    k_at = lax.broadcasted_iota(jnp.int32, (256, 256), 1)
    q_frame = (q_at >> 5) & 3
    k_frame = k_at >> 5
    tm = tm_ref[0]
    ok = (k_frame >= q_frame) & (k_frame <= q_frame + 4) & ((k_at & 31) < W)
    ok = ok & ((k_frame >= 2) | (tm > 0)) & ((k_frame < 6) | (tm < tm_ref[1] - 1))
    bias_s[...] = jnp.where(ok, 0.0, -1e30)
    lane = lax.broadcasted_iota(jnp.int32, (1, 128), 1)
    low = (lane < 64).astype(F32).astype(BF16)
    high = (lane >= 64).astype(F32).astype(BF16)
    low_lane = lane < 64

    def head_pair(it, carry):
        r = it // 4
        p = it % 4
        lanes = pl.ds(pl.multiple_of(p * 128, 128), 128)
        vlanes = pl.ds(pl.multiple_of(C + p * 128, 128), 128)
        q = qs[r, :, lanes]
        g = gs[r, :, lanes]
        k = kvs[r, :, lanes]
        v = kvs[r, :, vlanes]
        qq = jnp.concatenate([q * low, q * high], axis=0)
        gg = jnp.concatenate([g * low, g * high], axis=0)
        s = mm(qq, k, NT) + bias_s[...]
        gp = mm(gg, v, NT)
        e = jnp.exp(s - jnp.max(s, axis=1, keepdims=True))
        prob = e * (1.0 / jnp.sum(e, axis=1, keepdims=True))
        pb = prob.astype(BF16)
        pg = prob * gp
        ds = (pg - prob * jnp.sum(pg, axis=1, keepdims=True)).astype(BF16)
        o = mm(pb, v, NN)
        att_ref[r, :, lanes] = jnp.where(low_lane, o[:128], o[128:]).astype(BF16)
        dq = mm(ds, k, NN) * 0.125
        dq_ref[r, :, lanes] = jnp.where(low_lane, dq[:128], dq[128:]).astype(BF16)
        dk = mm(ds, qq, TN)
        dv = mm(pb, gg, TN)
        for value, at in ((dk, lanes), (dv, vlanes)):
            owed_prev_ref[r, :, at] = value[:64].astype(BF16)
            dkv_ref[r, :, at] = value[64:192]
            owed_next_ref[r, :, at] = value[192:].astype(BF16)
        return carry

    lax.fori_loop(0, 8, head_pair, 0)


def merge_kernel(att_ref, summed_ref, merge_ref, embed_w_ref, out_ref, embed_ref):
    for r in range(2):
        mixed = mm(att_ref[r], merge_ref[...], NN)
        block = (summed_ref[r] + mixed).astype(BF16)
        embed = mm(block, embed_w_ref[...], NN).astype(BF16)
        for f in range(4):
            out_ref[f, r] = block[f * WP : f * WP + W]
            embed_ref[f, r * WP : (r + 1) * WP, :] = embed[f * WP : (f + 1) * WP]


def grads_kernel(
    dkv_ref, from_prev_ref, from_next_ref, dq_ref, normed_ref, heads_ref, gain_ref, unit_ref,
    inv_ref, grad_ref, tokens_ref,
    out_ref, gp, shifts, red,
):
    for r in range(2):
        rows = slice(r * 128, (r + 1) * 128)
        gp[rows, 0:C] = dq_ref[r]
        gp[r * 128 : r * 128 + 64, C:] = (
            dkv_ref[r, 0:64, :] + from_prev_ref[r].astype(F32)
        ).astype(BF16)
        gp[r * 128 + 64 : (r + 1) * 128, C:] = (
            dkv_ref[r, 64:128, :] + from_next_ref[r].astype(F32)
        ).astype(BF16)

    col = lax.broadcasted_iota(jnp.int32, (C, C), 1)
    row = lax.broadcasted_iota(jnp.int32, (C, C), 0)
    source = ((col >> 4) & 15) * 32 + (col >> 8) * 16 + (col & 15)
    perm = (row == source).astype(F32).astype(BF16)
    normed = normed_ref[...].reshape(256, C)
    ordered = mm(normed, perm, NN).astype(BF16)
    for yh in range(4):
        part = mm(gp[:, yh * 384 : (yh + 1) * 384], ordered, TN).astype(BF16)
        for x in range(4):
            at = (x * 4 + yh) * 96
            for b in range(2):
                out_ref[b, at : at + 96, :] = part[x * 96 : (x + 1) * 96, b * 256 : (b + 1) * 256]

    gn = mm(gp[...], heads_ref[...], NT)
    unit = unit_ref[...].reshape(256, C)
    inv = inv_ref[...].reshape(256, 128)[:, 0:1]
    gu = gn * unit
    gain_sum = jnp.sum(gu.reshape(32, 8, C), axis=0)
    gain = gain_ref[...]
    scaled = gn * gain
    mean_a = jnp.sum(scaled, axis=1, keepdims=True) * (1.0 / C)
    mean_b = jnp.sum(gu * gain, axis=1, keepdims=True) * (1.0 / C)
    grad = grad_ref[...].reshape(256, C).astype(F32) + inv * (scaled - mean_a - unit * mean_b)
    keep = (lax.broadcasted_iota(jnp.int32, (256, 1), 0) & 31) < W
    grad = jnp.where(keep, grad, 0.0)
    for slab in range(8):
        piece = grad[slab * WP : (slab + 1) * WP]
        shifts[0, slab] = pltpu.roll(piece, WP - 1, 0)
        shifts[1, slab] = piece
        shifts[2, slab] = pltpu.roll(piece, 1, 0)

    def lane_chunk(c, carry):
        lanes = pl.ds(pl.multiple_of(c * 128, 128), 128)
        for dw in range(3):
            acc = [jnp.zeros((8, 128), F32) for _ in range(9)]
            for slab in range(8):
                r, f = slab // 4, slab % 4
                piece = shifts[dw, slab, :, lanes]
                for dt in range(3):
                    for dr in range(3):
                        token = tokens_ref[f + dt, r + dr, :, lanes].astype(F32)
                        prod = piece * token
                        acc[dt * 3 + dr] = acc[dt * 3 + dr] + (
                            (prod[0:8] + prod[8:16]) + (prod[16:24] + prod[24:32])
                        )
            for k in range(9):
                red[pl.ds((k * 3 + dw), 1), lanes] = jnp.sum(acc[k], axis=0, keepdims=True)
        return carry

    red[24:32, :] = jnp.zeros((8, C), F32)
    lax.fori_loop(0, 4, lane_chunk, 0)
    red[27:28, :] = jnp.sum(gain_sum, axis=0, keepdims=True)
    value = red[...]
    hi = value.astype(BF16)
    lo = (value - hi.astype(F32)).astype(BF16)
    for b in range(2):
        for half in range(2):
            at = slice(half * 256, (half + 1) * 256)
            out_ref[b, 1536 + half * 32 : 1568 + half * 32, :] = hi[:, at]
            out_ref[b, 1600 + half * 32 : 1632 + half * 32, :] = lo[:, at]


def split_pair(value):
    hi = value.astype(BF16)
    return hi, (value - hi.astype(F32)).astype(BF16)


def reduce_b_kernel(in_ref, out_ref):
    hi, lo = split_pair(
        (in_ref[0, 1536:1600].astype(F32) + in_ref[0, 1600:1664].astype(F32))
        + (in_ref[1, 1536:1600].astype(F32) + in_ref[1, 1600:1664].astype(F32))
    )
    for x in range(4):
        rows = slice(x * 384, (x + 1) * 384)
        out_ref[x, 0:384, :] = (
            in_ref[0, rows].astype(F32) + in_ref[1, rows].astype(F32)
        ).astype(BF16)
        out_ref[x, 384:448, :] = hi
        out_ref[x, 448:512, :] = lo


def reduce_x_kernel(in_ref, near_ref, embed_ref, match_ref, out_ref, info):
    parts = [in_ref[x].astype(F32) for x in range(4)]
    total = (parts[0] + parts[1]) + (parts[2] + parts[3])
    heads = jnp.transpose(total[0:384]).astype(BF16)
    small = total[384:448] + total[448:512]
    info[...] = jnp.zeros((16, 128), F32)
    for f in range(4):
        match = match_ref[f]
        row = (match * 2341) >> 16
        info[f * 2 : f * 2 + 2, 0:W] = row.astype(F32)
        info[8 + f * 2 : 10 + f * 2, 0:W] = (match - row * W).astype(F32)
    spot = lax.broadcasted_iota(jnp.int32, (64, 128), 0)
    lane = lax.broadcasted_iota(jnp.int32, (1, 128), 1)
    for q in range(16):
        for k in range(3):
            out_ref[q, k * 16 : k * 16 + 16, :] = heads[
                q * 16 : q * 16 + 16, k * 128 : (k + 1) * 128
            ]
        c = q // 4
        at = (c // 2) * 32 + (q % 4) * 8
        hi, lo = split_pair(small[at : at + 8, (c % 2) * 128 : (c % 2) * 128 + 128])
        out_ref[q, 48:64, :] = jnp.concatenate([hi, lo], axis=0)
        f, part = q % 4, q // 4
        where = []
        for k in range(2):
            line = info[k * 8 + f * 2 + part // 2 : k * 8 + f * 2 + part // 2 + 1, :]
            if part % 2:
                line = pltpu.roll(line, 112, 1)
            where.append(jnp.where(lane < 16, line, 0.0))
        rows = near_ref[f].astype(F32)
        rows = jnp.where(spot == 28, where[0], jnp.where(spot == 29, where[1], rows))
        out_ref[q, 64:128, :] = rows.astype(BF16)
        out_ref[q, 128:144, :] = embed_ref[f, part * 16 : part * 16 + 16, :]


def reduce_rows_kernel(in_ref, out_ref):
    total = in_ref[0, 0:64, :].astype(F32)
    for q in range(1, 16):
        total = total + in_ref[q, 0:64, :].astype(F32)
    heads = jnp.concatenate([total[0:16], total[16:32], total[32:48]], axis=1)
    small = total[48:56] + total[56:64]
    for yh in range(4):
        out_ref[yh, 0:16, 0:96] = heads[:, yh * 96 : (yh + 1) * 96]
        out_ref[yh, 0:16, 96:128] = jnp.zeros((16, 32), F32)
        out_ref[yh, 16:24, :] = small


def contrast_kernel(in_ref, out_ref):
    where = []
    for half in range(2):
        line = jnp.zeros((1, 128), F32)
        for k in range(8):
            tail = in_ref[half * 8 + k, 88:96, :].astype(F32)
            value = tail[4:5] * float(WP) + tail[5:6]
            line = line + (pltpu.roll(value, k * 16, 1) if k else value)
        where.append(line)
    where = jnp.concatenate(where, axis=1).astype(jnp.int32)
    at = lax.broadcasted_iota(jnp.int32, (1024, 256), 0)
    pick = (at == where).astype(F32).astype(BF16)
    table = in_ref[:, 64:128, :].reshape(1024, 128)
    found = mm(pick, table, TN)
    differ = in_ref[:, 128:144, :].reshape(256, 128).astype(F32) - found
    res = lax.dot_general(
        jnp.ones((8, 128), F32), differ * differ, NT,
        precision=lax.Precision.HIGHEST, preferred_element_type=F32,
    ) * (1.0 / 128.0)
    for q in range(16):
        line = res[:, (q // 8) * 128 : (q // 8) * 128 + 128]
        shift = (128 - (q % 8) * 16) % 128
        out_ref[q] = pltpu.roll(line, shift, 1) if shift else line


def reduce_y_kernel(in_ref, back_ref, heads_ref, out_ref):
    total = (in_ref[0] + in_ref[1]) + (in_ref[2] + in_ref[3])
    heads_ref[...] = total[0:16, 0:96]
    for q in range(16):
        out_ref[q, 0:8, :] = total[16:24]
        out_ref[q, 8:16, :] = back_ref[q]


def spread_kernel(in_ref, gain_ref, taps_ref, contrast_ref, tmp):
    for q in range(16):
        lanes = slice((q // 4) * 128, (q // 4) * 128 + 128)
        tmp[(q % 4) * 8 : (q % 4) * 8 + 8, lanes] = in_ref[q, 0:8, :]
    gain_ref[...] = tmp[27:28, :]
    taps_ref[...] = tmp[0:27, :]
    lane = lax.broadcasted_iota(jnp.int32, (1, 128), 1)
    for f in range(4):
        for r in range(2):
            even = in_ref[r * 8 + f, 8:9, :]
            odd = pltpu.roll(in_ref[r * 8 + 4 + f, 8:9, :], 16, 1)
            contrast_ref[f, r : r + 1, :] = jnp.where(lane < 16, even, odd)[:, 0:W]


def sds(shape, dtype):
    return jax.ShapeDtypeStruct(shape, dtype)


def smem():
    return pl.BlockSpec(memory_space=pltpu.SMEM)


def vmem():
    return pl.BlockSpec(memory_space=pltpu.VMEM)


def call(kernel, outs, ins, smem_first=False, scratch=(), name=None):
    specs = [vmem() for _ in ins]
    if smem_first:
        specs[0] = smem()
    return pl.pallas_call(
        kernel,
        out_shape=outs,
        in_specs=specs,
        out_specs=jax.tree.map(lambda _: vmem(), outs),
        scratch_shapes=list(scratch),
        compiler_params=pltpu.CompilerParams(vmem_limit_bytes=48 * 1024 * 1024),
        name=name,
    )(*ins)


def moved(block, axis, route):
    return lax.ppermute(block, axis, route)


def on_device(
    clip_tokens, conv_taps, norm_gain, heads_weight, merge_weight, embed_weight, matches, upstream
):
    tokens = clip_tokens[0]
    tm = lax.axis_index(TM)
    n_tm = lax.axis_size(TM)
    n_rows = lax.axis_size(ROWS)
    fwd = [(i, i + 1) for i in range(n_tm - 1)]
    back = [(i + 1, i) for i in range(n_tm - 1)]
    down = [(i, i + 1) for i in range(n_rows - 1)]
    up = [(i + 1, i) for i in range(n_rows - 1)]
    prev3 = moved(tokens[1:4], TM, fwd)
    next3 = moved(tokens[0:3], TM, back)
    last = jnp.concatenate([prev3[:, 1], tokens[:, 1], next3[:, 1]], axis=0)
    first = jnp.concatenate([prev3[:, 0], tokens[:, 0], next3[:, 0]], axis=0)
    above = moved(last, ROWS, down)
    below = moved(first, ROWS, up)
    gain = norm_gain.reshape(1, C)
    ups = upstream[0]
    where_tm = jnp.stack([tm, jnp.int32(n_tm)]).astype(jnp.int32)

    outs = (
        sds((2, 128, C), F32),
        sds((2, 128, C), F32),
        sds((2, 128, 128), F32),
        sds((2, 128, C), BF16),
        sds((6, 4, WP, C), BF16),
        sds((2, 128, C), BF16),
        sds((2, 128, C), BF16),
        sds((2, 128, C), BF16),
        sds((2, 128, 2 * C), F32),
        sds((2, 64, 2 * C), BF16),
        sds((2, 64, 2 * C), BF16),
    )
    summed, unit, inv, normed, tok6, grad, att, dq, dkv, owed_prev, owed_next = call(
        attend_kernel,
        outs,
        (where_tm, tokens, prev3, next3, above, below, conv_taps, gain, heads_weight,
         merge_weight, ups),
        smem_first=True,
        scratch=(
            pltpu.VMEM((10, 4, WP, C), F32),
            pltpu.VMEM((2, 256, C), BF16),
            pltpu.VMEM((2, 128, C), BF16),
            pltpu.VMEM((2, 256, 2 * C), BF16),
            pltpu.VMEM((2, 128, C), BF16),
            pltpu.VMEM((256, 256), F32),
        ),
        name="attend",
    )
    from_next = moved(owed_prev, TM, back)
    from_prev = moved(owed_next, TM, fwd)

    block_out, embed = call(
        merge_kernel,
        (sds((4, 2, W, C), BF16), sds((4, 64, 128), BF16)),
        (att, summed, merge_weight, embed_weight),
        name="merge",
    )
    from_next, from_prev, embed = lax.optimization_barrier((from_next, from_prev, embed))
    near = moved(embed, TM, [(i, (i - 1) % n_tm) for i in range(n_tm)])

    (stage,) = call(
        grads_kernel,
        (sds((2, 1664, 256), BF16),),
        (dkv, from_prev, from_next, dq, normed, heads_weight, gain, unit, inv, grad, tok6),
        scratch=(
            pltpu.VMEM((256, 3 * C), BF16),
            pltpu.VMEM((3, 8, WP, C), F32),
            pltpu.VMEM((32, C), F32),
        ),
        name="grads",
    )
    stage = lax.all_to_all(stage, "b", 0, 0, tiled=True)
    (stage,) = call(reduce_b_kernel, (sds((4, 512, 256), BF16),), (stage,), name="sum_b")
    stage = lax.all_to_all(stage, "x", 0, 0, tiled=True)
    (stage,) = call(
        reduce_x_kernel,
        (sds((16, 144, 128), BF16),),
        (stage, near, embed, matches[0]),
        scratch=(pltpu.VMEM((16, 128), F32),),
        name="sum_x",
    )
    stage = lax.all_to_all(stage, ROWS, 0, 0, tiled=True)
    (heads,) = call(reduce_rows_kernel, (sds((4, 24, 128), F32),), (stage,), name="sum_rows")
    heads = lax.all_to_all(heads, "yh", 0, 0, tiled=True)
    (back,) = call(contrast_kernel, (sds((16, 8, 128), F32),), (stage,), name="contrast")
    grad_heads, small = call(
        reduce_y_kernel,
        (sds((16, 96), F32), sds((16, 16, 128), F32)),
        (heads, back),
        name="sum_y",
    )
    small = lax.all_to_all(small, ROWS, 0, 0, tiled=True)
    grad_gain, grad_taps, contrast = call(
        spread_kernel,
        (sds((1, C), F32), sds((27, C), F32), sds((4, 2, W), F32)),
        (small,),
        scratch=(pltpu.VMEM((32, C), F32),),
        name="spread",
    )
    return (block_out[None], contrast[None], grad_heads, grad_gain.reshape(C), grad_taps)


def solution(mesh):
    fine = Mesh(
        np.asarray(mesh.devices).reshape(4, 4, 2, 8, 2), ("yh", "x", "yl", "z", "b")
    )
    placed = (
        P("b", TM, ROWS, None, None),
        P(),
        P(),
        P(),
        P(),
        P(),
        P("b", TM, ROWS, None),
        P("b", TM, ROWS, None, None),
    )
    return jax.shard_map(
        on_device,
        mesh=fine,
        in_specs=placed,
        out_specs=(
            P("b", TM, ROWS, None, None),
            P("b", TM, ROWS, None),
            P(("yl", "z", "b"), TM),
            P(),
            P(),
        ),
        check_vma=False,
    )
```

```python
import jax
import jax.numpy as jnp
import numpy as np
from jax import lax
from jax.experimental import pallas as pl
from jax.experimental.pallas import tpu as pltpu
from jax.sharding import Mesh, PartitionSpec as P

F32 = jnp.float32
BF16 = jnp.bfloat16
W = 28
WP = 32
C = 512
TM = ("yh", "x")
ROWS = ("yl", "z")

NN = (((1,), (0,)), ((), ()))
NT = (((1,), (1,)), ((), ()))
TN = (((0,), (0,)), ((), ()))


def mm(a, b, dims):
    return lax.dot_general(a, b, dims, preferred_element_type=F32)


def add_taps(acc, taps_ref, lanes, slab, dt, dr):
    for dw in range(3):
        tap = (dt * 3 + dr) * 3 + dw
        term = taps_ref[tap : tap + 1, lanes] * slab
        acc[dw] = term if acc[dw] is None else acc[dw] + term


def along_width(acc):
    return acc[1] + pltpu.roll(acc[0], 1, 0) + pltpu.roll(acc[2], WP - 1, 0)


def inner_kernel(
    own_ref, prev_ref, next_ref, taps_ref, upstream_ref, merge_ref,
    part_ref, tokens_ref, grad_ref, gatt_ref,
    xs,
):
    zeros_tail = jnp.zeros((8, C), F32)

    def place(f, r, slab):
        xs[f, r, 24:32, :] = zeros_tail
        xs[f, r, 0:W, :] = slab.astype(F32)

    for r in range(2):
        for f in range(3):
            place(f, r, prev_ref[f, r])
            place(7 + f, r, next_ref[f, r])
        for f in range(4):
            place(3 + f, r, own_ref[f, r])
        for f in range(6):
            tokens_ref[f, r] = xs[f + 2, r].astype(BF16)

    grad_ref[...] = jnp.zeros(grad_ref.shape, BF16)
    for f in range(4):
        for r in range(2):
            grad_ref[r, f * WP : f * WP + W, :] = upstream_ref[f, r]

    def conv_frame(f, carry):
        for c in range(4):
            lanes = slice(c * 128, (c + 1) * 128)
            accs = [[None] * 3, [None] * 3]
            for dt in range(3):
                for row in range(2):
                    slab = xs[f + dt, row, :, lanes]
                    for r in range(2):
                        add_taps(accs[r], taps_ref, lanes, slab, dt, row - r + 1)
            for r in range(2):
                part_ref[f, r, :, lanes] = xs[f + 1, r, :, lanes] + along_width(accs[r])
        return carry

    lax.fori_loop(0, 8, conv_frame, 0)
    for r in range(2):
        gatt_ref[r] = mm(grad_ref[r], merge_ref[...], NT).astype(BF16)


def attend_kernel(
    tm_ref, part_ref, up_ref, down_ref, taps_ref, gain_ref, heads_ref, gs,
    summed_ref, unit_ref, inv_ref, normed_ref, edge_ref, att_ref, dq_ref, dkv_ref,
    owed_prev_ref, owed_next_ref,
    xs, ns, qs, kvs, bias_s,
):
    zeros_tail = jnp.zeros((8, C), F32)
    for f in range(10):
        for r, ref in ((0, up_ref), (1, down_ref)):
            xs[f, r, 24:32, :] = zeros_tail
            xs[f, r, 0:W, :] = ref[f].astype(F32)
    for f in range(6):
        for r in range(2):
            edge_ref[f, r] = xs[f + 2, r].astype(BF16)

    keep = lax.broadcasted_iota(jnp.int32, (WP, 1), 0) < W

    def conv_frame(f, carry):
        for r in range(2):
            parts = []
            for c in range(4):
                lanes = slice(c * 128, (c + 1) * 128)
                acc = [None] * 3
                for dt in range(3):
                    add_taps(acc, taps_ref, lanes, xs[f + dt, r, :, lanes], dt, r * 2)
                parts.append(part_ref[f, r, :, lanes] + along_width(acc))
            summed = jnp.concatenate(parts, axis=1)
            mean = jnp.sum(summed, axis=1, keepdims=True) * (1.0 / C)
            centred = summed - mean
            var = jnp.sum(centred * centred, axis=1, keepdims=True) * (1.0 / C)
            inv = lax.rsqrt(var + 1e-05)
            unit = jnp.where(keep, centred * inv, 0.0)
            normed = (unit * gain_ref[...]).astype(BF16)
            ns[r, pl.ds(pl.multiple_of(f * WP, WP), WP), :] = normed

            @pl.when((f >= 2) & (f < 6))
            def _():
                rows = pl.ds(pl.multiple_of((f - 2) * WP, WP), WP)
                summed_ref[r, rows, :] = summed
                unit_ref[r, rows, :] = unit
                inv_ref[r, rows, :] = jnp.broadcast_to(inv, (WP, 128))

        return carry

    lax.fori_loop(0, 8, conv_frame, 0)

    for r in range(2):
        own = ns[r, 64:192, :]
        normed_ref[r] = own
        kvs[r] = mm(ns[r], heads_ref[:, C:], NN).astype(BF16)
        qs[r] = (mm(own, heads_ref[:, :C], NN).astype(BF16).astype(F32) * 0.125).astype(BF16)

    q_at = lax.broadcasted_iota(jnp.int32, (256, 256), 0)
    k_at = lax.broadcasted_iota(jnp.int32, (256, 256), 1)
    q_frame = (q_at >> 5) & 3
    k_frame = k_at >> 5
    tm = tm_ref[0]
    ok = (k_frame >= q_frame) & (k_frame <= q_frame + 4) & ((k_at & 31) < W)
    ok = ok & ((k_frame >= 2) | (tm > 0)) & ((k_frame < 6) | (tm < tm_ref[1] - 1))
    bias_s[...] = jnp.where(ok, 0.0, -1e30)
    lane = lax.broadcasted_iota(jnp.int32, (1, 128), 1)
    low = (lane < 64).astype(F32).astype(BF16)
    high = (lane >= 64).astype(F32).astype(BF16)
    low_lane = lane < 64

    def head_pair(it, carry):
        r = it // 4
        p = it % 4
        lanes = pl.ds(pl.multiple_of(p * 128, 128), 128)
        vlanes = pl.ds(pl.multiple_of(C + p * 128, 128), 128)
        q = qs[r, :, lanes]
        g = gs[r, :, lanes]
        k = kvs[r, :, lanes]
        v = kvs[r, :, vlanes]
        qq = jnp.concatenate([q * low, q * high], axis=0)
        gg = jnp.concatenate([g * low, g * high], axis=0)
        s = mm(qq, k, NT) + bias_s[...]
        gp = mm(gg, v, NT)
        e = jnp.exp(s - jnp.max(s, axis=1, keepdims=True))
        prob = e * (1.0 / jnp.sum(e, axis=1, keepdims=True))
        pb = prob.astype(BF16)
        pg = prob * gp
        ds = (pg - prob * jnp.sum(pg, axis=1, keepdims=True)).astype(BF16)
        o = mm(pb, v, NN)
        att_ref[r, :, lanes] = jnp.where(low_lane, o[:128], o[128:]).astype(BF16)
        dq = mm(ds, k, NN) * 0.125
        dq_ref[r, :, lanes] = jnp.where(low_lane, dq[:128], dq[128:]).astype(BF16)
        dk = mm(ds, qq, TN)
        dv = mm(pb, gg, TN)
        for value, at in ((dk, lanes), (dv, vlanes)):
            owed_prev_ref[r, :, at] = value[:64].astype(BF16)
            dkv_ref[r, :, at] = value[64:192]
            owed_next_ref[r, :, at] = value[192:].astype(BF16)
        return carry

    lax.fori_loop(0, 8, head_pair, 0, unroll=2)


def merge_kernel(att_ref, summed_ref, merge_ref, embed_w_ref, out_ref, embed_ref):
    for r in range(2):
        mixed = mm(att_ref[r], merge_ref[...], NN)
        block = (summed_ref[r] + mixed).astype(BF16)
        embed = mm(block, embed_w_ref[...], NN).astype(BF16)
        for f in range(4):
            out_ref[f, r] = block[f * WP : f * WP + W]
            embed_ref[f, r * WP : (r + 1) * WP, :] = embed[f * WP : (f + 1) * WP]


def query_kernel(dq_ref, normed_ref, heads_ref, ordered_ref, part_ref, gn_ref):
    col = lax.broadcasted_iota(jnp.int32, (C, C), 1)
    row = lax.broadcasted_iota(jnp.int32, (C, C), 0)
    source = ((col >> 4) & 15) * 32 + (col >> 8) * 16 + (col & 15)
    perm = (row == source).astype(F32).astype(BF16)
    ordered = mm(normed_ref[...].reshape(256, C), perm, NN).astype(BF16)
    ordered_ref[...] = ordered
    dq = dq_ref[...].reshape(256, C)
    part_ref[...] = mm(dq, ordered, TN).astype(BF16)
    gn_ref[...] = mm(dq, heads_ref[:, 0:C], NT)


def grads_kernel(
    dkv_ref, from_prev_ref, from_next_ref, ordered_ref, part_ref, gn_ref, heads_ref, gain_ref,
    unit_ref, inv_ref, grad_ref, mid_ref, edge_ref,
    out_ref, gp, shifts, red,
):
    for r in range(2):
        gp[r * 128 : r * 128 + 64, :] = (
            dkv_ref[r, 0:64, :] + from_prev_ref[r].astype(F32)
        ).astype(BF16)
        gp[r * 128 + 64 : (r + 1) * 128, :] = (
            dkv_ref[r, 64:128, :] + from_next_ref[r].astype(F32)
        ).astype(BF16)

    def put(piece, value):
        block, third = piece // 3, piece % 3
        at = ((block % 4) * 4 + block // 4) * 96 + third * 32
        for b in range(2):
            out_ref[b, at : at + 32, :] = value[:, b * 256 : (b + 1) * 256]

    for piece in range(16):
        put(piece, part_ref[piece * 32 : piece * 32 + 32, :])
    for quarter in range(4):
        part = mm(gp[:, quarter * 256 : (quarter + 1) * 256], ordered_ref[...], TN).astype(BF16)
        for k in range(8):
            put(16 + quarter * 8 + k, part[k * 32 : k * 32 + 32])

    gn = gn_ref[...] + mm(gp[...], heads_ref[:, C:], NT)
    unit = unit_ref[...].reshape(256, C)
    inv = inv_ref[...].reshape(256, 128)[:, 0:1]
    gu = gn * unit
    gain_sum = jnp.sum(gu.reshape(32, 8, C), axis=0)
    gain = gain_ref[...]
    scaled = gn * gain
    mean_a = jnp.sum(scaled, axis=1, keepdims=True) * (1.0 / C)
    mean_b = jnp.sum(gu * gain, axis=1, keepdims=True) * (1.0 / C)
    grad = grad_ref[...].reshape(256, C).astype(F32) + inv * (scaled - mean_a - unit * mean_b)
    keep = (lax.broadcasted_iota(jnp.int32, (256, 1), 0) & 31) < W
    grad = jnp.where(keep, grad, 0.0)
    for slab in range(8):
        piece = grad[slab * WP : (slab + 1) * WP]
        shifts[0, slab] = pltpu.roll(piece, WP - 1, 0)
        shifts[1, slab] = piece
        shifts[2, slab] = pltpu.roll(piece, 1, 0)

    def lane_chunk(c, carry):
        lanes = pl.ds(pl.multiple_of(c * 128, 128), 128)
        for dw in range(3):
            acc = [jnp.zeros((8, 128), F32) for _ in range(9)]
            for slab in range(8):
                r, f = slab // 4, slab % 4
                piece = shifts[dw, slab, :, lanes]
                for dt in range(3):
                    for dr in range(3):
                        at = r + dr
                        if at in (1, 2):
                            token = mid_ref[f + dt, at - 1, :, lanes].astype(F32)
                        else:
                            token = edge_ref[f + dt, at // 3, :, lanes].astype(F32)
                        prod = piece * token
                        acc[dt * 3 + dr] = acc[dt * 3 + dr] + (
                            (prod[0:8] + prod[8:16]) + (prod[16:24] + prod[24:32])
                        )
            for k in range(9):
                red[pl.ds((k * 3 + dw), 1), lanes] = jnp.sum(acc[k], axis=0, keepdims=True)
        return carry

    red[24:32, :] = jnp.zeros((8, C), F32)
    lax.fori_loop(0, 4, lane_chunk, 0)
    red[27:28, :] = jnp.sum(gain_sum, axis=0, keepdims=True)
    value = red[...]
    hi = value.astype(BF16)
    lo = (value - hi.astype(F32)).astype(BF16)
    for b in range(2):
        for half in range(2):
            at = slice(half * 256, (half + 1) * 256)
            out_ref[b, 1536 + half * 32 : 1568 + half * 32, :] = hi[:, at]
            out_ref[b, 1600 + half * 32 : 1632 + half * 32, :] = lo[:, at]


def split_pair(value):
    hi = value.astype(BF16)
    return hi, (value - hi.astype(F32)).astype(BF16)


def reduce_b_kernel(in_ref, out_ref):
    hi, lo = split_pair(
        (in_ref[0, 1536:1600].astype(F32) + in_ref[0, 1600:1664].astype(F32))
        + (in_ref[1, 1536:1600].astype(F32) + in_ref[1, 1600:1664].astype(F32))
    )
    for x in range(4):
        rows = slice(x * 384, (x + 1) * 384)
        out_ref[x, 0:384, :] = (
            in_ref[0, rows].astype(F32) + in_ref[1, rows].astype(F32)
        ).astype(BF16)
        out_ref[x, 384:448, :] = hi
        out_ref[x, 448:512, :] = lo


def reduce_x_kernel(in_ref, near_ref, embed_ref, match_ref, out_ref, info):
    parts = [in_ref[x].astype(F32) for x in range(4)]
    total = (parts[0] + parts[1]) + (parts[2] + parts[3])
    heads = jnp.transpose(total[0:384]).astype(BF16)
    small = total[384:448] + total[448:512]
    info[...] = jnp.zeros((16, 128), F32)
    for f in range(4):
        match = match_ref[f]
        row = (match * 2341) >> 16
        info[f * 2 : f * 2 + 2, 0:W] = row.astype(F32)
        info[8 + f * 2 : 10 + f * 2, 0:W] = (match - row * W).astype(F32)
    spot = lax.broadcasted_iota(jnp.int32, (64, 128), 0)
    lane = lax.broadcasted_iota(jnp.int32, (1, 128), 1)
    for q in range(16):
        for k in range(3):
            out_ref[q, k * 16 : k * 16 + 16, :] = heads[
                q * 16 : q * 16 + 16, k * 128 : (k + 1) * 128
            ]
        c = q // 4
        at = (c // 2) * 32 + (q % 4) * 8
        hi, lo = split_pair(small[at : at + 8, (c % 2) * 128 : (c % 2) * 128 + 128])
        out_ref[q, 48:64, :] = jnp.concatenate([hi, lo], axis=0)
        f, part = q % 4, q // 4
        where = []
        for k in range(2):
            line = info[k * 8 + f * 2 + part // 2 : k * 8 + f * 2 + part // 2 + 1, :]
            if part % 2:
                line = pltpu.roll(line, 112, 1)
            where.append(jnp.where(lane < 16, line, 0.0))
        rows = near_ref[f].astype(F32)
        rows = jnp.where(spot == 28, where[0], jnp.where(spot == 29, where[1], rows))
        out_ref[q, 64:128, :] = rows.astype(BF16)
        out_ref[q, 128:144, :] = embed_ref[f, part * 16 : part * 16 + 16, :]


def reduce_rows_kernel(in_ref, out_ref):
    total = in_ref[0, 0:64, :].astype(F32)
    for q in range(1, 16):
        total = total + in_ref[q, 0:64, :].astype(F32)
    heads = jnp.concatenate([total[0:16], total[16:32], total[32:48]], axis=1)
    small = total[48:56] + total[56:64]
    for yh in range(4):
        out_ref[yh, 0:16, 0:96] = heads[:, yh * 96 : (yh + 1) * 96]
        out_ref[yh, 0:16, 96:128] = jnp.zeros((16, 32), F32)
        out_ref[yh, 16:24, :] = small


def contrast_kernel(in_ref, out_ref):
    where = []
    for half in range(2):
        line = jnp.zeros((1, 128), F32)
        for k in range(8):
            tail = in_ref[half * 8 + k, 88:96, :].astype(F32)
            value = tail[4:5] * float(WP) + tail[5:6]
            line = line + (pltpu.roll(value, k * 16, 1) if k else value)
        where.append(line)
    where = jnp.concatenate(where, axis=1).astype(jnp.int32)
    at = lax.broadcasted_iota(jnp.int32, (1024, 256), 0)
    pick = (at == where).astype(F32).astype(BF16)
    table = in_ref[:, 64:128, :].reshape(1024, 128)
    found = mm(pick, table, TN)
    differ = in_ref[:, 128:144, :].reshape(256, 128).astype(F32) - found
    res = lax.dot_general(
        jnp.ones((8, 128), F32), differ * differ, NT,
        precision=lax.Precision.HIGHEST, preferred_element_type=F32,
    ) * (1.0 / 128.0)
    for q in range(16):
        line = res[:, (q // 8) * 128 : (q // 8) * 128 + 128]
        shift = (128 - (q % 8) * 16) % 128
        out_ref[q] = pltpu.roll(line, shift, 1) if shift else line


def reduce_y_kernel(in_ref, back_ref, heads_ref, out_ref):
    total = (in_ref[0] + in_ref[1]) + (in_ref[2] + in_ref[3])
    heads_ref[...] = total[0:16, 0:96]
    for q in range(16):
        out_ref[q, 0:8, :] = total[16:24]
        out_ref[q, 8:16, :] = back_ref[q]


def spread_kernel(in_ref, gain_ref, taps_ref, contrast_ref, tmp):
    for q in range(16):
        lanes = slice((q // 4) * 128, (q // 4) * 128 + 128)
        tmp[(q % 4) * 8 : (q % 4) * 8 + 8, lanes] = in_ref[q, 0:8, :]
    gain_ref[...] = tmp[27:28, :]
    taps_ref[...] = tmp[0:27, :]
    lane = lax.broadcasted_iota(jnp.int32, (1, 128), 1)
    for f in range(4):
        for r in range(2):
            even = in_ref[r * 8 + f, 8:9, :]
            odd = pltpu.roll(in_ref[r * 8 + 4 + f, 8:9, :], 16, 1)
            contrast_ref[f, r : r + 1, :] = jnp.where(lane < 16, even, odd)[:, 0:W]


def sds(shape, dtype):
    return jax.ShapeDtypeStruct(shape, dtype)


def smem():
    return pl.BlockSpec(memory_space=pltpu.SMEM)


def vmem():
    return pl.BlockSpec(memory_space=pltpu.VMEM)


def call(kernel, outs, ins, smem_first=False, scratch=(), name=None):
    specs = [vmem() for _ in ins]
    if smem_first:
        specs[0] = smem()
    return pl.pallas_call(
        kernel,
        out_shape=outs,
        in_specs=specs,
        out_specs=jax.tree.map(lambda _: vmem(), outs),
        scratch_shapes=list(scratch),
        compiler_params=pltpu.CompilerParams(vmem_limit_bytes=48 * 1024 * 1024),
        name=name,
    )(*ins)


def moved(block, axis, route):
    return lax.ppermute(block, axis, route)


def on_device(
    clip_tokens, conv_taps, norm_gain, heads_weight, merge_weight, embed_weight, matches, upstream
):
    tokens = clip_tokens[0]
    tm = lax.axis_index(TM)
    n_tm = lax.axis_size(TM)
    n_rows = lax.axis_size(ROWS)
    fwd = [(i, i + 1) for i in range(n_tm - 1)]
    back = [(i + 1, i) for i in range(n_tm - 1)]
    down = [(i, i + 1) for i in range(n_rows - 1)]
    up = [(i + 1, i) for i in range(n_rows - 1)]
    prev3 = moved(tokens[1:4], TM, fwd)
    next3 = moved(tokens[0:3], TM, back)
    last = jnp.concatenate([prev3[:, 1], tokens[:, 1], next3[:, 1]], axis=0)
    first = jnp.concatenate([prev3[:, 0], tokens[:, 0], next3[:, 0]], axis=0)
    above = moved(last, ROWS, down)
    below = moved(first, ROWS, up)
    gain = norm_gain.reshape(1, C)
    ups = upstream[0]
    where_tm = jnp.stack([tm, jnp.int32(n_tm)]).astype(jnp.int32)

    part, mid, grad, gatt = call(
        inner_kernel,
        (
            sds((8, 2, WP, C), F32),
            sds((6, 2, WP, C), BF16),
            sds((2, 128, C), BF16),
            sds((2, 128, C), BF16),
        ),
        (tokens, prev3, next3, conv_taps, ups, merge_weight),
        scratch=(pltpu.VMEM((10, 2, WP, C), F32),),
        name="inner",
    )
    outs = (
        sds((2, 128, C), F32),
        sds((2, 128, C), F32),
        sds((2, 128, 128), F32),
        sds((2, 128, C), BF16),
        sds((6, 2, WP, C), BF16),
        sds((2, 128, C), BF16),
        sds((2, 128, C), BF16),
        sds((2, 128, 2 * C), F32),
        sds((2, 64, 2 * C), BF16),
        sds((2, 64, 2 * C), BF16),
    )
    summed, unit, inv, normed, edge, att, dq, dkv, owed_prev, owed_next = call(
        attend_kernel,
        outs,
        (where_tm, part, above, below, conv_taps, gain, heads_weight, gatt),
        smem_first=True,
        scratch=(
            pltpu.VMEM((10, 2, WP, C), F32),
            pltpu.VMEM((2, 256, C), BF16),
            pltpu.VMEM((2, 128, C), BF16),
            pltpu.VMEM((2, 256, 2 * C), BF16),
            pltpu.VMEM((256, 256), F32),
        ),
        name="attend",
    )
    from_next = moved(owed_prev, TM, back)
    from_prev = moved(owed_next, TM, fwd)

    block_out, embed = call(
        merge_kernel,
        (sds((4, 2, W, C), BF16), sds((4, 64, 128), BF16)),
        (att, summed, merge_weight, embed_weight),
        name="merge",
    )
    near = moved(embed, TM, [(i, (i - 1) % n_tm) for i in range(n_tm)])
    ordered, t_query, gn_query = call(
        query_kernel,
        (sds((256, C), BF16), sds((C, C), BF16), sds((256, C), F32)),
        (dq, normed, heads_weight),
        name="query",
    )
    from_next, from_prev, near = lax.optimization_barrier((from_next, from_prev, near))
    (stage,) = call(
        grads_kernel,
        (sds((2, 1664, 256), BF16),),
        (dkv, from_prev, from_next, ordered, t_query, gn_query, heads_weight, gain, unit, inv,
         grad, mid, edge),
        scratch=(
            pltpu.VMEM((256, 2 * C), BF16),
            pltpu.VMEM((3, 8, WP, C), F32),
            pltpu.VMEM((32, C), F32),
        ),
        name="grads",
    )
    stage = lax.all_to_all(stage, "b", 0, 0, tiled=True)
    (stage,) = call(reduce_b_kernel, (sds((4, 512, 256), BF16),), (stage,), name="sum_b")
    stage = lax.all_to_all(stage, "x", 0, 0, tiled=True)
    (stage,) = call(
        reduce_x_kernel,
        (sds((16, 144, 128), BF16),),
        (stage, near, embed, matches[0]),
        scratch=(pltpu.VMEM((16, 128), F32),),
        name="sum_x",
    )
    stage = lax.all_to_all(stage, ROWS, 0, 0, tiled=True)
    (heads,) = call(reduce_rows_kernel, (sds((4, 24, 128), F32),), (stage,), name="sum_rows")
    heads = lax.all_to_all(heads, "yh", 0, 0, tiled=True)
    (back,) = call(contrast_kernel, (sds((16, 8, 128), F32),), (stage,), name="contrast")
    grad_heads, small = call(
        reduce_y_kernel,
        (sds((16, 96), F32), sds((16, 16, 128), F32)),
        (heads, back),
        name="sum_y",
    )
    small = lax.all_to_all(small, ROWS, 0, 0, tiled=True)
    grad_gain, grad_taps, contrast = call(
        spread_kernel,
        (sds((1, C), F32), sds((27, C), F32), sds((4, 2, W), F32)),
        (small,),
        scratch=(pltpu.VMEM((32, C), F32),),
        name="spread",
    )
    return (block_out[None], contrast[None], grad_heads, grad_gain.reshape(C), grad_taps)


def solution(mesh):
    fine = Mesh(
        np.asarray(mesh.devices).reshape(4, 4, 2, 8, 2), ("yh", "x", "yl", "z", "b")
    )
    placed = (
        P("b", TM, ROWS, None, None),
        P(),
        P(),
        P(),
        P(),
        P(),
        P("b", TM, ROWS, None),
        P("b", TM, ROWS, None, None),
    )
    return jax.shard_map(
        on_device,
        mesh=fine,
        in_specs=placed,
        out_specs=(
            P("b", TM, ROWS, None, None),
            P("b", TM, ROWS, None),
            P(("yl", "z", "b"), TM),
            P(),
            P(),
        ),
        check_vma=False,
    )
```
